32 devices in a mesh: sta: 16 (over z, x, core), strike: 2 (over y).
Axes of the slice: x: 2, y: 2, z: 4, core: 2. Of those that a mesh axis runs over, the one named last changes fastest.
Arguments:
- data: float32 [128, 512], P('sta'), may hold values from -6 to 6
- model: float32 [64, 64, 128], P(None, 'strike'), may hold values from -6 to 6
- green: bfloat16 [16, 2, 96, 128, 128], P('sta', 'strike'), may hold values from -0.03125 to 0.03125
- block_ids: int32 [16, 2, 96], P('sta', 'strike'), may hold values from -1 to 1023, as said below
Outputs:
- residual: float32 [128, 512], P('sta')
- updated: float32 [64, 64, 128], P(None, 'strike')
The draws below stay inside these ranges and needn't reach their ends.
Inputs may be any that keep to these rules, and one draw needn't show every extreme that they name: In each block_ids[g, h] the ids that are not -1 are distinct and stand in the first slots; every pair uses at least a third of its 96 slots, and in every draw some pair uses all 96.
All inputs are finite; a program needn't handle non-finite values.
Results may differ from the reference program's by a relative error of at most 0.0023.
Values sent between devices are 32-bit elements; how exact they have to be, the bound alone decides.
A program may use at most 64 MiB of HBM per device.

```python
import jax
import jax.numpy as jnp
from jax import lax

BLOCK = 128
W = 64
DIP = 128
SWEEPS = 4
STA_DEV = 8
SAMPLES = 512
S_DEV = 32
CAP = 96
STA_GROUPS = 16
PATCH_GROUPS = 2
STATIONS = 128
STRIKE_CELLS = 64
TB = 4
NRB = 32
N_STA = 16
N_STRIKE = 2


def draw_block_ids(key, part):
    groups = STA_GROUPS * PATCH_GROUPS
    total = NRB * S_DEV
    key_perm, key_count, key_full = jax.random.split(jax.random.fold_in(key, 17), 3)
    perms = jax.vmap(lambda one_key: jax.random.permutation(one_key, total))(jax.random.split(key_perm, groups))
    perms = perms[:, :CAP]
    counts = jax.random.randint(key_count, (groups,), (CAP + 2) // 3, CAP + 1)
    fullest = jax.random.randint(key_full, (), 0, groups)
    counts = jnp.where(jnp.arange(groups) == fullest, CAP, counts)
    slots = jnp.arange(CAP)
    chosen = jnp.where(slots[None, :] < counts[:, None], perms, -1)
    return chosen.reshape(STA_GROUPS, PATCH_GROUPS, CAP).astype(jnp.int32)


def block_levels(stream_key, extent, shards, least, top_value):
    factor_of = 1.0
    for position, shards_of in shards:
        draws = jax.random.uniform(jax.random.fold_in(jax.random.fold_in(stream_key, 6), position), (shards_of,), jnp.float32, least / len(shards), top_value / len(shards))
        factor_of = factor_of * jnp.repeat(jnp.exp(draws), extent[position] // shards_of).reshape((-1,) + (1,) * (len(extent) - 1 - position))
    return factor_of


def noise(rng, dims, width, most, cuts=(), kind=jnp.bfloat16):
    result = width * jax.random.normal(rng, dims, jnp.float32)
    if cuts:
        result = result * block_levels(rng, dims, cuts, -0.22, 0.18)
    return jnp.clip(result, -most, most).astype(kind)


def setup_inputs(seed: int = 0) -> dict:
    splits = jax.random.split(jax.random.key(seed), 5)
    data = noise(splits[0], (STATIONS, SAMPLES), 1.0, 6.0, ((0, 16),), jnp.float32)
    model = noise(splits[1], (W, STRIKE_CELLS, DIP), 1.0, 6.0, ((1, 2),), jnp.float32)
    green = noise(splits[2], (STA_GROUPS, PATCH_GROUPS, CAP, BLOCK, BLOCK), (2 * N_STRIKE * DIP * W) ** -0.5, 0.03125, ((0, 16), (1, 2)))
    block_ids = draw_block_ids(jax.random.fold_in(splits[4], 71), 0)
    return dict(data=data, model=model, green=green, block_ids=block_ids)


NU_DIFF = 0.1
STEP_LEN = 4.0


def shear_add(series):
    count_rows, windows, length = series.shape
    padded = jnp.pad(series, ((0, 0), (0, 0), (0, windows)))
    flattened = padded.reshape(count_rows, windows * (length + windows))[:, : windows * (length + windows - 1)]
    sheared = flattened.reshape(count_rows, windows, length + windows - 1)
    return jnp.sum(sheared[:, :, :length], axis=1)


def shear_take(residual, windows):
    count_rows, length = residual.shape
    padded = jnp.pad(residual, ((0, 0), (0, windows)))
    repeated = jnp.broadcast_to(padded[:, None, :], (count_rows, windows, length + windows))
    repeated = repeated.reshape(count_rows, windows * (length + windows))
    repeated = jnp.pad(repeated, ((0, 0), (0, windows)))
    return repeated.reshape(count_rows, windows, length + windows + 1)[:, :, :length]


def slot_layout(slot_ids):
    usable = slot_ids >= 0
    safe_ids = jnp.where(usable, slot_ids, 0).astype(jnp.int32)
    return usable, safe_ids // S_DEV, safe_ids % S_DEV


def forward_partial(green_dev, slot_ids, model_dev):
    usable, row_block, col_block = slot_layout(slot_ids)
    columns = jnp.take(model_dev, col_block, axis=1).astype(jnp.float32)
    products = jnp.einsum('cts,wcs->cwt', green_dev.astype(jnp.float32), columns, precision=lax.Precision.HIGHEST)
    picks = ((row_block[None, :] == jnp.arange(NRB, dtype=jnp.int32)[:, None]) & usable[None, :]).astype(jnp.float32)
    gathered = jnp.einsum('rc,cwt->rwt', picks, products, precision=lax.Precision.HIGHEST)
    series = gathered.reshape(STA_DEV, TB, W, BLOCK).transpose(0, 2, 1, 3).reshape(STA_DEV, W, SAMPLES)
    return shear_add(series)


def adjoint_partial(green_dev, slot_ids, resid_group):
    usable, row_block, col_block = slot_layout(slot_ids)
    shifted = shear_take(resid_group, W)
    row_blocks = shifted.reshape(STA_DEV, W, TB, BLOCK).transpose(0, 2, 1, 3).reshape(NRB, W, BLOCK)
    res_rows = jnp.take(row_blocks, row_block, axis=0).astype(jnp.float32)
    slot_grads = jnp.einsum('cts,cwt->cws', green_dev.astype(jnp.float32), res_rows, precision=lax.Precision.HIGHEST)
    picks = ((col_block[None, :] == jnp.arange(S_DEV, dtype=jnp.int32)[:, None]) & usable[None, :]).astype(jnp.float32)
    return jnp.einsum('pc,cws->wps', picks, slot_grads, precision=lax.Precision.HIGHEST)


def reference(data, model, green, block_ids):
    model_bf = model.astype(jnp.bfloat16)
    model_parts = model_bf.reshape(W, N_STRIKE, S_DEV, DIP).transpose(1, 0, 2, 3)

    def synth_group(pieces):
        green_row, ids_row = pieces
        return jnp.sum(jax.vmap(forward_partial)(green_row, ids_row, model_parts), axis=0)

    synthetic = lax.map(synth_group, (green, block_ids)).reshape(STATIONS, SAMPLES)
    residual = synthetic - data
    resid_bf = residual.astype(jnp.bfloat16).reshape(N_STA, STA_DEV, SAMPLES)

    def grad_step(total, pieces):
        green_row, ids_row, resid_group = pieces
        terms = jax.vmap(adjoint_partial, in_axes=(0, 0, None))(green_row, ids_row, resid_group)
        return total + terms, None

    start = jnp.zeros((N_STRIKE, W, S_DEV, DIP), jnp.float32)
    total, unused = lax.scan(grad_step, start, (green, block_ids, resid_bf))
    field = total.transpose(1, 0, 2, 3).reshape(W, STRIKE_CELLS, DIP)
    for sweep in range(SWEEPS):
        padded = jnp.pad(field, ((0, 0), (1, 1), (1, 1)))
        laplace = padded[:, 2:, 1:-1] + padded[:, :-2, 1:-1] + padded[:, 1:-1, 2:] + padded[:, 1:-1, :-2] - 4.0 * field
        field = field + NU_DIFF * laplace
    return residual, model - STEP_LEN * field
```

```python
import functools

import jax
import jax.numpy as jnp
from jax import lax
from jax.experimental import pallas as pl
from jax.experimental.pallas import tpu as pltpu
from jax.sharding import PartitionSpec as P

SWEEPS = 4
NU_DIFF = 0.1
STEP_LEN = 4.0
MESH = pl.DeviceIdType.MESH
CHUNKS = 6
HALO = 8


def green_copy(green_ref, gbuf, sems, i, size):
    return pltpu.make_async_copy(
        green_ref.at[pl.ds(i * size, size)], gbuf.at[pl.ds(i * size, size)], sems.at[i]
    )


def forward_kernel(strike_rows, ids_ref, model_ref, green_ref, out_ref, gbuf, cols, prod, acc, sems):
    slots, block = gbuf.shape[:2]
    windows = cols.shape[1]
    sta_rows, samples = out_ref.shape
    time_blocks = samples // block
    row_count = sta_rows * time_blocks
    size = slots // CHUNKS
    for i in range(CHUNKS):
        green_copy(green_ref, gbuf, sems, i, size).start()
    acc[...] = jnp.zeros_like(acc)
    for q in range(strike_rows):
        cols[q] = model_ref[pl.ds(q, windows, stride=strike_rows), :].astype(jnp.bfloat16)

    @pl.loop(0, CHUNKS)
    def _(i):
        green_copy(green_ref, gbuf, sems, i, size).wait()
        for u in range(size):
            c = i * size + u
            q = lax.rem(jnp.maximum(ids_ref[c], 0), strike_rows)
            prod[c] = lax.dot_general(
                cols[q], gbuf[c], (((1,), (1,)), ((), ())), preferred_element_type=jnp.float32
            )

    @pl.loop(0, slots, step=4)
    def _(base):
        for u in range(4):
            slot_id = ids_ref[base + u]
            row = jnp.where(slot_id >= 0, lax.div(jnp.maximum(slot_id, 0), strike_rows), row_count)
            acc[row] = acc[row] + prod[base + u]

    window = lax.broadcasted_iota(jnp.int32, (windows, block), 0)
    lane = lax.broadcasted_iota(jnp.int32, (windows, block), 1)
    same = lane >= window
    for a in range(sta_rows):
        before = jnp.zeros((windows, block), jnp.float32)
        for b in range(time_blocks):
            rolled = pltpu.roll(acc[a * time_blocks + b], 0, 1, stride=1, stride_axis=0)
            out_ref[a : a + 1, b * block : (b + 1) * block] = jnp.sum(
                jnp.where(same, rolled, before), axis=0, keepdims=True
            )
            before = rolled


def adjoint_kernel(strike_rows, ids_ref, resid_ref, green_ref, out_ref, gbuf, rows, prod, acc, sems):
    slots, block = gbuf.shape[:2]
    windows = rows.shape[1]
    sta_rows, samples = resid_ref.shape
    time_blocks = samples // block
    size = slots // CHUNKS
    for i in range(CHUNKS):
        green_copy(green_ref, gbuf, sems, i, size).start()
    acc[...] = jnp.zeros_like(acc)
    back = windows - 1 - lax.broadcasted_iota(jnp.int32, (windows, block), 0)
    same = lax.broadcasted_iota(jnp.int32, (windows, block), 1) + back < block
    for a in range(sta_rows):
        after = jnp.zeros((windows, block), jnp.float32)
        for b in reversed(range(time_blocks)):
            line = jnp.broadcast_to(resid_ref[a : a + 1, b * block : (b + 1) * block], (windows, block))
            rolled = pltpu.roll(line, block - windows + 1, 1, stride=1, stride_axis=0)
            rows[a * time_blocks + b] = jnp.where(same, rolled, after).astype(jnp.bfloat16)
            after = rolled

    @pl.loop(0, CHUNKS)
    def _(i):
        green_copy(green_ref, gbuf, sems, i, size).wait()
        for u in range(size):
            c = i * size + u
            row = lax.div(jnp.maximum(ids_ref[c], 0), strike_rows)
            prod[c] = jnp.dot(rows[row], gbuf[c], preferred_element_type=jnp.float32)

    @pl.loop(0, slots, step=4)
    def _(base):
        for u in range(4):
            slot_id = ids_ref[base + u]
            q = jnp.where(slot_id >= 0, lax.rem(jnp.maximum(slot_id, 0), strike_rows), strike_rows)
            here = pl.ds(pl.multiple_of(q * windows, windows), windows)
            acc[here, :] = acc[here, :] + prod[base + u]

    for w in range(windows):
        out_ref[w * strike_rows : (w + 1) * strike_rows, :] = acc[
            pl.ds(windows - 1 - w, strike_rows, stride=windows), :
        ]


def exchange_kernel(n, part_ref, data_ref, out_ref, parts, send, recv):
    me = lax.axis_index("strike")
    barrier = pltpu.get_barrier_semaphore()
    for d in range(1, n):
        pl.semaphore_signal(
            barrier, inc=1, device_id={"strike": lax.rem(me + d, n)}, device_id_type=MESH
        )
    pl.semaphore_wait(barrier, n - 1)
    copies = []
    for d in range(1, n):
        copy = pltpu.make_async_remote_copy(
            src_ref=part_ref,
            dst_ref=parts.at[d],
            send_sem=send.at[d],
            recv_sem=recv.at[d],
            device_id={"strike": lax.rem(me + d, n)},
            device_id_type=MESH,
        )
        copy.start()
        copies.append(copy)
    parts[0] = part_ref[...]
    for copy in copies:
        copy.wait()
    total = parts[lax.rem(me, n)]
    for j in range(1, n):
        total = total + parts[lax.rem(me - j + n, n)]
    out_ref[...] = total - data_ref[...]


def reduce_kernel(
    n_sta, n_strike, pieces, grad_ref, model_ref, out_ref, from_core, from_x, from_z, ext,
    core_s, core_r, x_s, x_r, z_s, z_r, halo_s, halo_r, gz_s, gz_r, gx_s, gx_r, gc_s, gc_r,
):
    depth = n_sta // 4
    own = grad_ref.shape[3]
    rows, dip = grad_ref.shape[4:]
    part = own // pieces
    sta = lax.axis_index("sta")
    strike = lax.axis_index("strike")
    core = lax.rem(sta, 2)
    x = lax.rem(lax.div(sta, 2), 2)
    z = lax.div(sta, 4)
    other_core, other_x = 1 - core, 1 - x
    core_dev = {"sta": z * 4 + x * 2 + other_core}
    x_dev = {"sta": z * 4 + other_x * 2 + core}

    def z_at(d):
        return lax.rem(z + d, depth)

    def z_dev(d):
        return {"sta": z_at(d) * 4 + x * 2 + core}

    up_dev = {"strike": lax.rem(strike + 1, n_strike)}
    down_dev = {"strike": lax.rem(strike + n_strike - 1, n_strike)}
    peers = [core_dev, x_dev] + [z_dev(d) for d in range(1, depth)] + [up_dev, down_dev]
    barrier = pltpu.get_barrier_semaphore()
    for peer in peers:
        pl.semaphore_signal(barrier, inc=1, device_id=peer, device_id_type=MESH)
    pl.semaphore_wait(barrier, len(peers))

    started = []

    def send(src, dst, s, r, dev):
        copy = pltpu.make_async_remote_copy(
            src_ref=src, dst_ref=dst, send_sem=s, recv_sem=r, device_id=dev, device_id_type=MESH
        )
        copy.start()
        started.append(copy)
        return copy

    def cut(k):
        return pl.ds(k * part, part)

    halves = []
    for h, side in enumerate((other_x, x)):
        for k in range(pieces):
            halves.append(
                send(
                    grad_ref.at[other_core, side, :, cut(k)],
                    from_core.at[h, :, cut(k)],
                    core_s.at[h, k],
                    core_r.at[h, k],
                    core_dev,
                )
            )
    across = []
    for k in range(pieces):
        halves[k].wait_recv()
        from_core[0, :, cut(k)] = from_core[0, :, cut(k)] + grad_ref[core, other_x, :, cut(k)]
        across.append(
            send(from_core.at[0, :, cut(k)], from_x.at[:, cut(k)], x_s.at[k], x_r.at[k], x_dev)
        )
    for k in range(pieces):
        halves[pieces + k].wait_recv()
        from_core[1, :, cut(k)] = from_core[1, :, cut(k)] + grad_ref[core, x, :, cut(k)]
    along = []
    for k in range(pieces):
        across[k].wait_recv()
        from_x[:, cut(k)] = from_x[:, cut(k)] + from_core[1, :, cut(k)]
        for d in range(1, depth):
            along.append(
                send(
                    from_x.at[z_at(d), cut(k)],
                    from_z.at[d - 1, cut(k)],
                    z_s.at[d - 1, k],
                    z_r.at[d - 1, k],
                    z_dev(d),
                )
            )
    for copy in along:
        copy.wait_recv()
    field = from_x[z]
    for d in range(1, depth):
        field = field + from_z[d - 1]

    ext[:, HALO : HALO + rows] = field
    high = send(
        ext.at[:, pl.ds(rows, HALO)], ext.at[:, pl.ds(0, HALO)], halo_s.at[0], halo_r.at[0], up_dev
    )
    low = send(
        ext.at[:, pl.ds(HALO, HALO)],
        ext.at[:, pl.ds(HALO + rows, HALO)],
        halo_s.at[1],
        halo_r.at[1],
        down_dev,
    )
    tall = rows + 2 * HALO
    row = lax.broadcasted_iota(jnp.int32, (own, tall, dip), 1)
    lane = lax.broadcasted_iota(jnp.int32, (own, tall, dip), 2)
    first = jnp.where(strike > 0, 0, HALO)
    last = jnp.where(strike < n_strike - 1, tall, HALO + rows)
    inside = (row >= first) & (row < last)
    high.wait_recv()
    low.wait_recv()
    v = jnp.where(inside, ext[...], 0.0)
    for _ in range(SWEEPS):
        left = jnp.where(lane > 0, pltpu.roll(v, 1, 2), 0.0)
        right = jnp.where(lane < dip - 1, pltpu.roll(v, dip - 1, 2), 0.0)
        around = pltpu.roll(v, tall - 1, 1) + pltpu.roll(v, 1, 1) + right + left - 4.0 * v
        v = jnp.where(inside, v + NU_DIFF * around, 0.0)
    out_ref[core, x, z] = model_ref[core, x, z] - STEP_LEN * v[:, HALO : HALO + rows]

    mine = out_ref.at[core, x, z]
    fetched = [send(mine, mine, gz_s.at[d], gz_r.at[d], z_dev(d)) for d in range(1, depth)]
    crossed = []
    to_core = []
    for d in range(depth):
        if d:
            fetched[d - 1].wait_recv()
        block = out_ref.at[core, x, lax.rem(z - d + depth, depth)]
        crossed.append(send(block, block, gx_s.at[d], gx_r.at[d], x_dev))
        to_core.append(send(block, block, gc_s.at[0, d], gc_r.at[0, d], core_dev))
    for d in range(depth):
        crossed[d].wait_recv()
        block = out_ref.at[core, other_x, lax.rem(z - d + depth, depth)]
        to_core.append(send(block, block, gc_s.at[1, d], gc_r.at[1, d], core_dev))
    for copy in to_core:
        copy.wait_recv()
    for copy in started:
        copy.wait_send()


def local(n_sta, n_strike, data, model, green, block_ids):
    sta_rows, samples = data.shape
    windows, strike_rows, dip = model.shape
    slots, block = green.shape[2], green.shape[3]
    row_count = sta_rows * (samples // block)
    green = green.reshape(green.shape[2:])
    ids = block_ids.reshape(-1)
    vmem = pl.BlockSpec(memory_space=pltpu.VMEM)
    smem = pl.BlockSpec(memory_space=pltpu.SMEM)
    hbm = pl.BlockSpec(memory_space=pl.ANY)
    f32 = jnp.float32
    dma = pltpu.SemaphoreType.DMA

    partial = pl.pallas_call(
        functools.partial(forward_kernel, strike_rows),
        out_shape=jax.ShapeDtypeStruct((sta_rows, samples), f32),
        in_specs=[smem, vmem, hbm],
        out_specs=vmem,
        scratch_shapes=[
            pltpu.VMEM((slots, block, dip), green.dtype),
            pltpu.VMEM((strike_rows, windows, dip), jnp.bfloat16),
            pltpu.VMEM((slots, windows, block), f32),
            pltpu.VMEM((row_count + 1, windows, block), f32),
            dma((CHUNKS,)),
        ],
        name="forward",
    )(ids, model.reshape(windows * strike_rows, dip), green)

    residual = pl.pallas_call(
        functools.partial(exchange_kernel, n_strike),
        out_shape=jax.ShapeDtypeStruct((sta_rows, samples), f32),
        in_specs=[vmem, vmem],
        out_specs=vmem,
        scratch_shapes=[
            pltpu.VMEM((n_strike, sta_rows, samples), f32),
            dma((n_strike,)),
            dma((n_strike,)),
        ],
        compiler_params=pltpu.CompilerParams(collective_id=0, has_side_effects=True),
        name="exchange",
    )(partial, data)

    grad = pl.pallas_call(
        functools.partial(adjoint_kernel, strike_rows),
        out_shape=jax.ShapeDtypeStruct((windows * strike_rows, dip), f32),
        in_specs=[smem, vmem, hbm],
        out_specs=vmem,
        scratch_shapes=[
            pltpu.VMEM((slots, block, dip), green.dtype),
            pltpu.VMEM((row_count, windows, block), jnp.bfloat16),
            pltpu.VMEM((slots, windows, dip), f32),
            pltpu.VMEM(((strike_rows + 1) * windows, dip), f32),
            dma((CHUNKS,)),
        ],
        name="adjoint",
    )(ids, residual, green)

    depth = n_sta // 4
    own = windows // n_sta
    pieces = min(own, 4)
    parted = (2, 2, depth, own, strike_rows, dip)
    updated = pl.pallas_call(
        functools.partial(reduce_kernel, n_sta, n_strike, pieces),
        out_shape=jax.ShapeDtypeStruct(parted, f32),
        in_specs=[vmem, vmem],
        out_specs=vmem,
        scratch_shapes=[
            pltpu.VMEM((2,) + parted[2:], f32),
            pltpu.VMEM(parted[2:], f32),
            pltpu.VMEM((depth - 1,) + parted[3:], f32),
            pltpu.VMEM((own, strike_rows + 2 * HALO, dip), f32),
            dma((2, pieces)), dma((2, pieces)),
            dma((pieces,)), dma((pieces,)),
            dma((depth - 1, pieces)), dma((depth - 1, pieces)),
            dma((2,)), dma((2,)),
            dma((depth,)), dma((depth,)),
            dma((depth,)), dma((depth,)),
            dma((2, depth)), dma((2, depth)),
        ],
        compiler_params=pltpu.CompilerParams(collective_id=1, has_side_effects=True),
        name="reduce",
    )(grad.reshape(parted), model.reshape(parted))
    return residual, updated.reshape(windows, strike_rows, dip)


def solution(mesh):
    in_specs = (
        P("sta", None),
        P(None, "strike", None),
        P("sta", "strike", None, None, None),
        P("sta", "strike", None),
    )
    out_specs = (P("sta", None), P(None, "strike", None))
    body = functools.partial(local, mesh.shape["sta"], mesh.shape["strike"])
    return jax.shard_map(body, mesh=mesh, in_specs=in_specs, out_specs=out_specs, check_vma=False)
```

```python
import functools

import jax
import jax.numpy as jnp
from jax import lax
from jax.experimental import pallas as pl
from jax.experimental.pallas import tpu as pltpu
from jax.sharding import PartitionSpec as P

SWEEPS = 4
NU_DIFF = 0.1
STEP_LEN = 4.0
MESH = pl.DeviceIdType.MESH
CHUNKS = 6
HALO = 8
VMEM_LIMIT = 16 * 2**20


def green_copy(green_ref, gbuf, sems, i, size):
    return pltpu.make_async_copy(
        green_ref.at[pl.ds(i * size, size)], gbuf.at[pl.ds(i * size, size)], sems.at[i]
    )


def forward_kernel(strike_rows, ids_ref, model_hbm, green_ref, out_ref, model_ref, gbuf, cols, prod, acc, model_sem, sems):
    slots, block = gbuf.shape[:2]
    windows = cols.shape[1]
    sta_rows, samples = out_ref.shape
    time_blocks = samples // block
    row_count = sta_rows * time_blocks
    size = slots // CHUNKS
    model_copy = pltpu.make_async_copy(model_hbm, model_ref, model_sem)
    model_copy.start()
    for i in range(CHUNKS):
        green_copy(green_ref, gbuf, sems, i, size).start()
    acc[...] = jnp.zeros_like(acc)
    model_copy.wait()
    for q in range(strike_rows):
        cols[q] = model_ref[pl.ds(q, windows, stride=strike_rows), :].astype(jnp.bfloat16)

    @pl.loop(0, CHUNKS)
    def _(i):
        green_copy(green_ref, gbuf, sems, i, size).wait()
        for u in range(size):
            c = i * size + u
            q = lax.rem(jnp.maximum(ids_ref[c], 0), strike_rows)
            prod[c] = lax.dot_general(
                cols[q], gbuf[c], (((1,), (1,)), ((), ())), preferred_element_type=jnp.float32
            )

    @pl.loop(0, slots, step=4)
    def _(base):
        for u in range(4):
            slot_id = ids_ref[base + u]
            row = jnp.where(slot_id >= 0, lax.div(jnp.maximum(slot_id, 0), strike_rows), row_count)
            acc[row] = acc[row] + prod[base + u]

    window = lax.broadcasted_iota(jnp.int32, (windows, block), 0)
    lane = lax.broadcasted_iota(jnp.int32, (windows, block), 1)
    same = lane >= window
    for a in range(sta_rows):
        before = jnp.zeros((windows, block), jnp.float32)
        for b in range(time_blocks):
            rolled = pltpu.roll(acc[a * time_blocks + b], 0, 1, stride=1, stride_axis=0)
            out_ref[a : a + 1, b * block : (b + 1) * block] = jnp.sum(
                jnp.where(same, rolled, before), axis=0, keepdims=True
            )
            before = rolled


def adjoint_kernel(strike_rows, ids_ref, resid_ref, green_ref, out_ref, rows, prod, acc):
    slots, block = green_ref.shape[:2]
    windows = rows.shape[1]
    sta_rows, samples = resid_ref.shape
    time_blocks = samples // block
    size = slots // CHUNKS
    acc[...] = jnp.zeros_like(acc)
    back = windows - 1 - lax.broadcasted_iota(jnp.int32, (windows, block), 0)
    same = lax.broadcasted_iota(jnp.int32, (windows, block), 1) + back < block
    for a in range(sta_rows):
        after = jnp.zeros((windows, block), jnp.float32)
        for b in reversed(range(time_blocks)):
            line = jnp.broadcast_to(resid_ref[a : a + 1, b * block : (b + 1) * block], (windows, block))
            rolled = pltpu.roll(line, block - windows + 1, 1, stride=1, stride_axis=0)
            rows[a * time_blocks + b] = jnp.where(same, rolled, after).astype(jnp.bfloat16)
            after = rolled

    @pl.loop(0, CHUNKS)
    def _(i):
        for u in range(size):
            c = i * size + u
            row = lax.div(jnp.maximum(ids_ref[c], 0), strike_rows)
            prod[c] = jnp.dot(rows[row], green_ref[c], preferred_element_type=jnp.float32)

    @pl.loop(0, slots, step=4)
    def _(base):
        for u in range(4):
            slot_id = ids_ref[base + u]
            q = jnp.where(slot_id >= 0, lax.rem(jnp.maximum(slot_id, 0), strike_rows), strike_rows)
            here = pl.ds(pl.multiple_of(q * windows, windows), windows)
            acc[here, :] = acc[here, :] + prod[base + u]

    for w in range(windows):
        out_ref[w * strike_rows : (w + 1) * strike_rows, :] = acc[
            pl.ds(windows - 1 - w, strike_rows, stride=windows), :
        ]


def exchange_kernel(n, part_ref, data_ref, out_ref, parts, send, recv):
    me = lax.axis_index("strike")
    barrier = pltpu.get_barrier_semaphore()
    for d in range(1, n):
        pl.semaphore_signal(
            barrier, inc=1, device_id={"strike": lax.rem(me + d, n)}, device_id_type=MESH
        )
    pl.semaphore_wait(barrier, n - 1)
    copies = []
    for d in range(1, n):
        copy = pltpu.make_async_remote_copy(
            src_ref=part_ref,
            dst_ref=parts.at[d],
            send_sem=send.at[d],
            recv_sem=recv.at[d],
            device_id={"strike": lax.rem(me + d, n)},
            device_id_type=MESH,
        )
        copy.start()
        copies.append(copy)
    parts[0] = part_ref[...]
    for copy in copies:
        copy.wait()
    total = parts[lax.rem(me, n)]
    for j in range(1, n):
        total = total + parts[lax.rem(me - j + n, n)]
    out_ref[...] = total - data_ref[...]


def reduce_kernel(
    n_sta, n_strike, pieces, grad_ref, out_ref, from_core, from_x, from_z, ext,
    core_s, core_r, x_s, x_r, z_s, z_r, halo_s, halo_r, gz_s, gz_r, gx_s, gx_r, gc_s, gc_r,
):
    depth = n_sta // 4
    own = grad_ref.shape[3]
    rows, dip = grad_ref.shape[4:]
    part = own // pieces
    sta = lax.axis_index("sta")
    strike = lax.axis_index("strike")
    core = lax.rem(sta, 2)
    x = lax.rem(lax.div(sta, 2), 2)
    z = lax.div(sta, 4)
    other_core, other_x = 1 - core, 1 - x
    core_dev = {"sta": z * 4 + x * 2 + other_core}
    x_dev = {"sta": z * 4 + other_x * 2 + core}

    def z_at(d):
        return lax.rem(z + d, depth)

    def z_dev(d):
        return {"sta": z_at(d) * 4 + x * 2 + core}

    up_dev = {"strike": lax.rem(strike + 1, n_strike)}
    down_dev = {"strike": lax.rem(strike + n_strike - 1, n_strike)}
    peers = [core_dev, x_dev] + [z_dev(d) for d in range(1, depth)] + [up_dev, down_dev]
    barrier = pltpu.get_barrier_semaphore()
    for peer in peers:
        pl.semaphore_signal(barrier, inc=1, device_id=peer, device_id_type=MESH)
    pl.semaphore_wait(barrier, len(peers))

    started = []

    def send(src, dst, s, r, dev):
        copy = pltpu.make_async_remote_copy(
            src_ref=src, dst_ref=dst, send_sem=s, recv_sem=r, device_id=dev, device_id_type=MESH
        )
        copy.start()
        started.append(copy)
        return copy

    def cut(k):
        return pl.ds(k * part, part)

    halves = []
    for h, side in enumerate((other_x, x)):
        for k in range(pieces):
            halves.append(
                send(
                    grad_ref.at[other_core, side, :, cut(k)],
                    from_core.at[h, :, cut(k)],
                    core_s.at[h, k],
                    core_r.at[h, k],
                    core_dev,
                )
            )
    across = []
    for k in range(pieces):
        halves[k].wait_recv()
        from_core[0, :, cut(k)] = from_core[0, :, cut(k)] + grad_ref[core, other_x, :, cut(k)]
        across.append(
            send(from_core.at[0, :, cut(k)], from_x.at[:, cut(k)], x_s.at[k], x_r.at[k], x_dev)
        )
    for k in range(pieces):
        halves[pieces + k].wait_recv()
        from_core[1, :, cut(k)] = from_core[1, :, cut(k)] + grad_ref[core, x, :, cut(k)]
    along = []
    for k in range(pieces):
        across[k].wait_recv()
        from_x[:, cut(k)] = from_x[:, cut(k)] + from_core[1, :, cut(k)]
        for d in range(1, depth):
            along.append(
                send(
                    from_x.at[z_at(d), cut(k)],
                    from_z.at[d - 1, cut(k)],
                    z_s.at[d - 1, k],
                    z_r.at[d - 1, k],
                    z_dev(d),
                )
            )
    for copy in along:
        copy.wait_recv()
    field = from_x[z]
    for d in range(1, depth):
        field = field + from_z[d - 1]

    ext[:, HALO : HALO + rows] = field
    high = send(
        ext.at[:, pl.ds(rows, HALO)], ext.at[:, pl.ds(0, HALO)], halo_s.at[0], halo_r.at[0], up_dev
    )
    low = send(
        ext.at[:, pl.ds(HALO, HALO)],
        ext.at[:, pl.ds(HALO + rows, HALO)],
        halo_s.at[1],
        halo_r.at[1],
        down_dev,
    )

    def diffuse(v, inside):
        tall = v.shape[1]
        lane = lax.broadcasted_iota(jnp.int32, v.shape, 2)
        for _ in range(SWEEPS):
            left = jnp.where(lane > 0, pltpu.roll(v, 1, 2), 0.0)
            right = jnp.where(lane < dip - 1, pltpu.roll(v, dip - 1, 2), 0.0)
            around = pltpu.roll(v, tall - 1, 1) + pltpu.roll(v, 1, 1) + right + left - 4.0 * v
            v = v + NU_DIFF * around
            if inside is not None:
                v = jnp.where(inside, v, 0.0)
        return v

    mid = diffuse(field, None)
    out_ref[core, x, z, :, HALO : rows - HALO] = STEP_LEN * mid[:, HALO : rows - HALO]

    spans = ((HALO, rows - 2 * HALO), (0, HALO), (rows - HALO, HALO))

    def view(a, b, c, j):
        return out_ref.at[a, b, c, :, pl.ds(*spans[j])]

    fetched, crossed, to_core = {}, {}, []

    def give(j, d):
        block = view(core, x, lax.rem(z - d + depth, depth), j)
        crossed[j, d] = send(block, block, gx_s.at[j, d], gx_r.at[j, d], x_dev)
        to_core.append(send(block, block, gc_s.at[0, j, d], gc_r.at[0, j, d], core_dev))

    def spread(j):
        block = view(core, x, z, j)
        for d in range(1, depth):
            fetched[j, d] = send(block, block, gz_s.at[j, d], gz_r.at[j, d], z_dev(d))
        give(j, 0)

    spread(0)
    high.wait_recv()
    low.wait_recv()
    for j, start in ((1, 0), (2, rows - HALO)):
        strip = ext[:, start : start + 3 * HALO]
        row = lax.broadcasted_iota(jnp.int32, strip.shape, 1)
        if j == 1:
            inside = row >= jnp.where(strike > 0, 0, HALO)
        else:
            inside = row < jnp.where(strike < n_strike - 1, 3 * HALO, 2 * HALO)
        strip = diffuse(jnp.where(inside, strip, 0.0), inside)
        out_ref[core, x, z, :, spans[j][0] : spans[j][0] + HALO] = STEP_LEN * strip[:, HALO : 2 * HALO]
        spread(j)
    for j in range(3):
        for d in range(1, depth):
            fetched[j, d].wait_recv()
            give(j, d)
    for j in range(3):
        for d in range(depth):
            crossed[j, d].wait_recv()
            block = view(core, other_x, lax.rem(z - d + depth, depth), j)
            to_core.append(send(block, block, gc_s.at[1, j, d], gc_r.at[1, j, d], core_dev))
    for copy in to_core:
        copy.wait_recv()
    for copy in started:
        copy.wait_send()


def local(n_sta, n_strike, data, model, green, block_ids):
    sta_rows, samples = data.shape
    windows, strike_rows, dip = model.shape
    slots, block = green.shape[2], green.shape[3]
    row_count = sta_rows * (samples // block)
    green = green.reshape(green.shape[2:])
    ids = block_ids.reshape(-1)
    vmem = pl.BlockSpec(memory_space=pltpu.VMEM)
    smem = pl.BlockSpec(memory_space=pltpu.SMEM)
    hbm = pl.BlockSpec(memory_space=pl.ANY)
    f32 = jnp.float32
    dma = pltpu.SemaphoreType.DMA

    partial = pl.pallas_call(
        functools.partial(forward_kernel, strike_rows),
        out_shape=jax.ShapeDtypeStruct((sta_rows, samples), f32),
        in_specs=[smem, hbm, hbm],
        out_specs=vmem,
        scratch_shapes=[
            pltpu.VMEM((windows * strike_rows, dip), f32),
            pltpu.VMEM((slots, block, dip), green.dtype),
            pltpu.VMEM((strike_rows, windows, dip), jnp.bfloat16),
            pltpu.VMEM((slots, windows, block), f32),
            pltpu.VMEM((row_count + 1, windows, block), f32),
            dma,
            dma((CHUNKS,)),
        ],
        name="forward",
    )(ids, model.reshape(windows * strike_rows, dip), green)

    residual = pl.pallas_call(
        functools.partial(exchange_kernel, n_strike),
        out_shape=jax.ShapeDtypeStruct((sta_rows, samples), f32),
        in_specs=[vmem, vmem],
        out_specs=vmem,
        scratch_shapes=[
            pltpu.VMEM((n_strike, sta_rows, samples), f32),
            dma((n_strike,)),
            dma((n_strike,)),
        ],
        compiler_params=pltpu.CompilerParams(collective_id=0, has_side_effects=True, vmem_limit_bytes=VMEM_LIMIT),
        name="exchange",
    )(partial, data)

    grad = pl.pallas_call(
        functools.partial(adjoint_kernel, strike_rows),
        out_shape=jax.ShapeDtypeStruct((windows * strike_rows, dip), f32),
        in_specs=[smem, vmem, vmem],
        out_specs=vmem,
        scratch_shapes=[
            pltpu.VMEM((row_count, windows, block), jnp.bfloat16),
            pltpu.VMEM((slots, windows, dip), f32),
            pltpu.VMEM(((strike_rows + 1) * windows, dip), f32),
        ],
        compiler_params=pltpu.CompilerParams(vmem_limit_bytes=VMEM_LIMIT),
        name="adjoint",
    )(ids, residual, green)

    depth = n_sta // 4
    own = windows // n_sta
    pieces = min(own, 4)
    parted = (2, 2, depth, own, strike_rows, dip)
    field = pl.pallas_call(
        functools.partial(reduce_kernel, n_sta, n_strike, pieces),
        out_shape=jax.ShapeDtypeStruct(parted, f32),
        in_specs=[vmem],
        out_specs=vmem,
        scratch_shapes=[
            pltpu.VMEM((2,) + parted[2:], f32),
            pltpu.VMEM(parted[2:], f32),
            pltpu.VMEM((depth - 1,) + parted[3:], f32),
            pltpu.VMEM((own, strike_rows + 2 * HALO, dip), f32),
            dma((2, pieces)), dma((2, pieces)),
            dma((pieces,)), dma((pieces,)),
            dma((depth - 1, pieces)), dma((depth - 1, pieces)),
            dma((2,)), dma((2,)),
            dma((3, depth)), dma((3, depth)),
            dma((3, depth)), dma((3, depth)),
            dma((2, 3, depth)), dma((2, 3, depth)),
        ],
        compiler_params=pltpu.CompilerParams(collective_id=1, has_side_effects=True, vmem_limit_bytes=VMEM_LIMIT),
        name="reduce",
    )(grad.reshape(parted))
    updated = model - field.reshape(windows, strike_rows, dip)
    return residual, updated


def solution(mesh):
    in_specs = (
        P("sta", None),
        P(None, "strike", None),
        P("sta", "strike", None, None, None),
        P("sta", "strike", None),
    )
    out_specs = (P("sta", None), P(None, "strike", None))
    body = functools.partial(local, mesh.shape["sta"], mesh.shape["strike"])
    return jax.shard_map(body, mesh=mesh, in_specs=in_specs, out_specs=out_specs, check_vma=False)
```

```python
import functools

import jax
import jax.numpy as jnp
from jax import lax
from jax.experimental import pallas as pl
from jax.experimental.pallas import tpu as pltpu
from jax.sharding import PartitionSpec as P

SWEEPS = 4
NU_DIFF = 0.1
STEP_LEN = 4.0
MESH = pl.DeviceIdType.MESH
CHUNKS = 6
HALO = 8
VMEM_LIMIT = 16 * 2**20


def green_copy(green_ref, gbuf, sems, i, size):
    return pltpu.make_async_copy(
        green_ref.at[pl.ds(i * size, size)], gbuf.at[pl.ds(i * size, size)], sems.at[i]
    )


def forward_kernel(strike_rows, ids_ref, model_hbm, green_ref, out_ref, gbuf, model_ref, cols, prod, acc, model_sem, sems):
    slots, block = gbuf.shape[:2]
    windows = cols.shape[1]
    sta_rows, samples = out_ref.shape
    time_blocks = samples // block
    row_count = sta_rows * time_blocks
    size = slots // CHUNKS
    model_copy = pltpu.make_async_copy(model_hbm, model_ref, model_sem)
    model_copy.start()
    for i in range(CHUNKS):
        green_copy(green_ref, gbuf, sems, i, size).start()
    acc[...] = jnp.zeros_like(acc)
    model_copy.wait()
    for q in range(strike_rows):
        cols[q] = model_ref[pl.ds(q, windows, stride=strike_rows), :].astype(jnp.bfloat16)

    @pl.loop(0, CHUNKS)
    def _(i):
        green_copy(green_ref, gbuf, sems, i, size).wait()
        for u in range(size):
            c = i * size + u
            q = lax.rem(jnp.maximum(ids_ref[c], 0), strike_rows)
            prod[c] = lax.dot_general(
                cols[q], gbuf[c], (((1,), (1,)), ((), ())), preferred_element_type=jnp.float32
            )

    @pl.loop(0, slots, step=4)
    def _(base):
        for u in range(4):
            slot_id = ids_ref[base + u]
            row = jnp.where(slot_id >= 0, lax.div(jnp.maximum(slot_id, 0), strike_rows), row_count)
            acc[row] = acc[row] + prod[base + u]

    window = lax.broadcasted_iota(jnp.int32, (windows, block), 0)
    lane = lax.broadcasted_iota(jnp.int32, (windows, block), 1)
    same = lane >= window
    for a in range(sta_rows):
        before = jnp.zeros((windows, block), jnp.float32)
        for b in range(time_blocks):
            rolled = pltpu.roll(acc[a * time_blocks + b], 0, 1, stride=1, stride_axis=0)
            out_ref[a : a + 1, b * block : (b + 1) * block] = jnp.sum(
                jnp.where(same, rolled, before), axis=0, keepdims=True
            )
            before = rolled


def adjoint_kernel(strike_rows, ids_ref, synth_ref, data_ref, green_ref, resid_ref, acc, rows, prod):
    slots, block = green_ref.shape[:2]
    windows = rows.shape[1]
    sta_rows, samples = resid_ref.shape
    time_blocks = samples // block
    size = slots // CHUNKS
    resid_ref[...] = synth_ref[...] - data_ref[...]
    acc[...] = jnp.zeros_like(acc)
    back = windows - 1 - lax.broadcasted_iota(jnp.int32, (windows, block), 0)
    same = lax.broadcasted_iota(jnp.int32, (windows, block), 1) + back < block
    for a in range(sta_rows):
        after = jnp.zeros((windows, block), jnp.float32)
        for b in reversed(range(time_blocks)):
            line = jnp.broadcast_to(resid_ref[a : a + 1, b * block : (b + 1) * block], (windows, block))
            rolled = pltpu.roll(line, block - windows + 1, 1, stride=1, stride_axis=0)
            rows[a * time_blocks + b] = jnp.where(same, rolled, after).astype(jnp.bfloat16)
            after = rolled

    @pl.loop(0, CHUNKS)
    def _(i):
        for u in range(size):
            c = i * size + u
            row = lax.div(jnp.maximum(ids_ref[c], 0), strike_rows)
            prod[c] = jnp.dot(rows[row], green_ref[c], preferred_element_type=jnp.float32)

    @pl.loop(0, slots, step=4)
    def _(base):
        for u in range(4):
            slot_id = ids_ref[base + u]
            q = jnp.where(slot_id >= 0, lax.rem(jnp.maximum(slot_id, 0), strike_rows), strike_rows)
            here = pl.ds(pl.multiple_of(q * windows, windows), windows)
            acc[here, :] = acc[here, :] + prod[base + u]


def exchange_kernel(n, part_ref, out_ref, parts, send, recv):
    me = lax.axis_index("strike")
    barrier = pltpu.get_barrier_semaphore()
    for d in range(1, n):
        pl.semaphore_signal(
            barrier, inc=1, device_id={"strike": lax.rem(me + d, n)}, device_id_type=MESH
        )
    pl.semaphore_wait(barrier, n - 1)
    copies = []
    for d in range(1, n):
        copy = pltpu.make_async_remote_copy(
            src_ref=part_ref,
            dst_ref=parts.at[d],
            send_sem=send.at[d],
            recv_sem=recv.at[d],
            device_id={"strike": lax.rem(me + d, n)},
            device_id_type=MESH,
        )
        copy.start()
        copies.append(copy)
    parts[0] = part_ref[...]
    for copy in copies:
        copy.wait()
    total = parts[lax.rem(me, n)]
    for j in range(1, n):
        total = total + parts[lax.rem(me - j + n, n)]
    out_ref[...] = total


def reduce_kernel(
    n_sta, n_strike, acc_ref, out_ref, grad_ref, from_core, from_x, from_z, ext,
    core_s, core_r, x_s, x_r, z_s, z_r, halo_s, halo_r, gz_s, gz_r, gx_s, gx_r, gc_s, gc_r,
):
    depth = n_sta // 4
    own = grad_ref.shape[3]
    halves_of_rows = 2
    pieces = own * halves_of_rows
    rows, dip = grad_ref.shape[4:]
    part = rows // halves_of_rows
    sta = lax.axis_index("sta")
    strike = lax.axis_index("strike")
    core = lax.rem(sta, 2)
    x = lax.rem(lax.div(sta, 2), 2)
    z = lax.div(sta, 4)
    other_core, other_x = 1 - core, 1 - x
    core_dev = {"sta": z * 4 + x * 2 + other_core}
    x_dev = {"sta": z * 4 + other_x * 2 + core}

    def z_at(d):
        return lax.rem(z + d, depth)

    def z_dev(d):
        return {"sta": z_at(d) * 4 + x * 2 + core}

    up_dev = {"strike": lax.rem(strike + 1, n_strike)}
    down_dev = {"strike": lax.rem(strike + n_strike - 1, n_strike)}
    peers = [core_dev, x_dev] + [z_dev(d) for d in range(1, depth)] + [up_dev, down_dev]
    barrier = pltpu.get_barrier_semaphore()
    for peer in peers:
        pl.semaphore_signal(barrier, inc=1, device_id=peer, device_id_type=MESH)
    windows = 4 * depth * own
    for w in range(windows):
        place = (w // (windows // 2), w // (windows // 4) % 2, w // own % depth, w % own)
        grad_ref[place] = acc_ref[pl.ds(windows - 1 - w, rows, stride=windows), :]
    pl.semaphore_wait(barrier, len(peers))

    started = []

    def send(src, dst, s, r, dev):
        copy = pltpu.make_async_remote_copy(
            src_ref=src, dst_ref=dst, send_sem=s, recv_sem=r, device_id=dev, device_id_type=MESH
        )
        copy.start()
        started.append(copy)
        return copy

    def cut(k):
        return (pl.ds(k // halves_of_rows, 1), pl.ds(k % halves_of_rows * part, part))

    halves = []
    for h, side in enumerate((other_x, x)):
        for k in range(pieces):
            halves.append(
                send(
                    grad_ref.at[other_core, side, :, *cut(k)],
                    from_core.at[h, :, *cut(k)],
                    core_s.at[h, k],
                    core_r.at[h, k],
                    core_dev,
                )
            )
    across = []
    for k in range(pieces):
        halves[k].wait_recv()
        from_core[0, :, *cut(k)] = from_core[0, :, *cut(k)] + grad_ref[core, other_x, :, *cut(k)]
        across.append(
            send(from_core.at[0, :, *cut(k)], from_x.at[:, *cut(k)], x_s.at[k], x_r.at[k], x_dev)
        )
    for k in range(pieces):
        halves[pieces + k].wait_recv()
        from_core[1, :, *cut(k)] = from_core[1, :, *cut(k)] + grad_ref[core, x, :, *cut(k)]
    along = []
    for k in range(pieces):
        across[k].wait_recv()
        from_x[:, *cut(k)] = from_x[:, *cut(k)] + from_core[1, :, *cut(k)]
        for d in range(1, depth):
            along.append(
                send(
                    from_x.at[z_at(d), *cut(k)],
                    from_z.at[d - 1, *cut(k)],
                    z_s.at[d - 1, k],
                    z_r.at[d - 1, k],
                    z_dev(d),
                )
            )
    for copy in along:
        copy.wait_recv()
    field = from_x[z]
    for d in range(1, depth):
        field = field + from_z[d - 1]

    ext[:, HALO : HALO + rows] = field
    high = send(
        ext.at[:, pl.ds(rows, HALO)], ext.at[:, pl.ds(0, HALO)], halo_s.at[0], halo_r.at[0], up_dev
    )
    low = send(
        ext.at[:, pl.ds(HALO, HALO)],
        ext.at[:, pl.ds(HALO + rows, HALO)],
        halo_s.at[1],
        halo_r.at[1],
        down_dev,
    )

    def diffuse(v, inside):
        tall = v.shape[1]
        lane = lax.broadcasted_iota(jnp.int32, v.shape, 2)
        for _ in range(SWEEPS):
            left = jnp.where(lane > 0, pltpu.roll(v, 1, 2), 0.0)
            right = jnp.where(lane < dip - 1, pltpu.roll(v, dip - 1, 2), 0.0)
            around = pltpu.roll(v, tall - 1, 1) + pltpu.roll(v, 1, 1) + right + left - 4.0 * v
            v = v + NU_DIFF * around
            if inside is not None:
                v = jnp.where(inside, v, 0.0)
        return v

    mid = diffuse(field, None)
    out_ref[core, x, z, :, HALO : rows - HALO] = STEP_LEN * mid[:, HALO : rows - HALO]

    spans = ((HALO, rows - 2 * HALO), (0, HALO), (rows - HALO, HALO))

    def view(a, b, c, j):
        return out_ref.at[a, b, c, :, pl.ds(*spans[j])]

    fetched, crossed, to_core = {}, {}, []

    def give(j, d):
        block = view(core, x, lax.rem(z - d + depth, depth), j)
        crossed[j, d] = send(block, block, gx_s.at[j, d], gx_r.at[j, d], x_dev)
        to_core.append(send(block, block, gc_s.at[0, j, d], gc_r.at[0, j, d], core_dev))

    def spread(j):
        block = view(core, x, z, j)
        for d in range(1, depth):
            fetched[j, d] = send(block, block, gz_s.at[j, d], gz_r.at[j, d], z_dev(d))
        give(j, 0)

    spread(0)
    high.wait_recv()
    low.wait_recv()
    for j, start in ((1, 0), (2, rows - HALO)):
        strip = ext[:, start : start + 3 * HALO]
        row = lax.broadcasted_iota(jnp.int32, strip.shape, 1)
        if j == 1:
            inside = row >= jnp.where(strike > 0, 0, HALO)
        else:
            inside = row < jnp.where(strike < n_strike - 1, 3 * HALO, 2 * HALO)
        strip = diffuse(jnp.where(inside, strip, 0.0), inside)
        out_ref[core, x, z, :, spans[j][0] : spans[j][0] + HALO] = STEP_LEN * strip[:, HALO : 2 * HALO]
        spread(j)
    for j in range(3):
        for d in range(1, depth):
            fetched[j, d].wait_recv()
            give(j, d)
    for j in range(3):
        for d in range(depth):
            crossed[j, d].wait_recv()
            block = view(core, other_x, lax.rem(z - d + depth, depth), j)
            to_core.append(send(block, block, gc_s.at[1, j, d], gc_r.at[1, j, d], core_dev))
    for copy in to_core:
        copy.wait_recv()
    for copy in started:
        copy.wait_send()


def local(n_sta, n_strike, data, model, green, block_ids):
    sta_rows, samples = data.shape
    windows, strike_rows, dip = model.shape
    slots, block = green.shape[2], green.shape[3]
    row_count = sta_rows * (samples // block)
    green = green.reshape(green.shape[2:])
    ids = block_ids.reshape(-1)
    vmem = pl.BlockSpec(memory_space=pltpu.VMEM)
    smem = pl.BlockSpec(memory_space=pltpu.SMEM)
    hbm = pl.BlockSpec(memory_space=pl.ANY)
    f32 = jnp.float32
    dma = pltpu.SemaphoreType.DMA

    partial, green = pl.pallas_call(
        functools.partial(forward_kernel, strike_rows),
        out_shape=(
            jax.ShapeDtypeStruct((sta_rows, samples), f32),
            jax.ShapeDtypeStruct((slots, block, dip), green.dtype),
        ),
        in_specs=[smem, hbm, hbm],
        out_specs=(vmem, vmem),
        scratch_shapes=[
            pltpu.VMEM((windows * strike_rows, dip), f32),
            pltpu.VMEM((strike_rows, windows, dip), jnp.bfloat16),
            pltpu.VMEM((slots, windows, block), f32),
            pltpu.VMEM((row_count + 1, windows, block), f32),
            dma,
            dma((CHUNKS,)),
        ],
        compiler_params=pltpu.CompilerParams(vmem_limit_bytes=VMEM_LIMIT),
        name="forward",
    )(
        ids,
        pltpu.with_memory_space_constraint(model.reshape(windows * strike_rows, dip), pltpu.HBM),
        pltpu.with_memory_space_constraint(green, pltpu.HBM),
    )

    synthetic = pl.pallas_call(
        functools.partial(exchange_kernel, n_strike),
        out_shape=jax.ShapeDtypeStruct((sta_rows, samples), f32),
        in_specs=[vmem],
        out_specs=vmem,
        scratch_shapes=[
            pltpu.VMEM((n_strike, sta_rows, samples), f32),
            dma((n_strike,)),
            dma((n_strike,)),
        ],
        compiler_params=pltpu.CompilerParams(collective_id=0, has_side_effects=True, vmem_limit_bytes=VMEM_LIMIT),
        name="exchange",
    )(partial)

    residual, grad = pl.pallas_call(
        functools.partial(adjoint_kernel, strike_rows),
        out_shape=(
            jax.ShapeDtypeStruct((sta_rows, samples), f32),
            jax.ShapeDtypeStruct(((strike_rows + 1) * windows, dip), f32),
        ),
        in_specs=[smem, vmem, vmem, vmem],
        out_specs=(vmem, vmem),
        scratch_shapes=[
            pltpu.VMEM((row_count, windows, block), jnp.bfloat16),
            pltpu.VMEM((slots, windows, dip), f32),
        ],
        compiler_params=pltpu.CompilerParams(vmem_limit_bytes=VMEM_LIMIT),
        name="adjoint",
    )(ids, synthetic, data, green)

    depth = n_sta // 4
    own = windows // n_sta
    pieces = 2 * own
    parted = (2, 2, depth, own, strike_rows, dip)
    field = pl.pallas_call(
        functools.partial(reduce_kernel, n_sta, n_strike),
        out_shape=jax.ShapeDtypeStruct(parted, f32),
        in_specs=[vmem],
        out_specs=vmem,
        scratch_shapes=[
            pltpu.VMEM(parted, f32),
            pltpu.VMEM((2,) + parted[2:], f32),
            pltpu.VMEM(parted[2:], f32),
            pltpu.VMEM((depth - 1,) + parted[3:], f32),
            pltpu.VMEM((own, strike_rows + 2 * HALO, dip), f32),
            dma((2, pieces)), dma((2, pieces)),
            dma((pieces,)), dma((pieces,)),
            dma((depth - 1, pieces)), dma((depth - 1, pieces)),
            dma((2,)), dma((2,)),
            dma((3, depth)), dma((3, depth)),
            dma((3, depth)), dma((3, depth)),
            dma((2, 3, depth)), dma((2, 3, depth)),
        ],
        compiler_params=pltpu.CompilerParams(collective_id=1, has_side_effects=True, vmem_limit_bytes=VMEM_LIMIT),
        name="reduce",
    )(grad)
    updated = model - field.reshape(windows, strike_rows, dip)
    return residual, updated


def solution(mesh):
    in_specs = (
        P("sta", None),
        P(None, "strike", None),
        P("sta", "strike", None, None, None),
        P("sta", "strike", None),
    )
    out_specs = (P("sta", None), P(None, "strike", None))
    body = functools.partial(local, mesh.shape["sta"], mesh.shape["strike"])
    return jax.shard_map(body, mesh=mesh, in_specs=in_specs, out_specs=out_specs, check_vma=False)
```

```python
import functools

import jax
import jax.numpy as jnp
from jax import lax
from jax.experimental import pallas as pl
from jax.experimental.pallas import tpu as pltpu
from jax.sharding import PartitionSpec as P

SWEEPS = 4
NU_DIFF = 0.1
STEP_LEN = 4.0
MESH = pl.DeviceIdType.MESH
CHUNKS = 6
HALO = 8
VMEM_LIMIT = 16 * 2**20


def green_copy(green_ref, gbuf, sems, i, size):
    return pltpu.make_async_copy(
        green_ref.at[pl.ds(i * size, size)], gbuf.at[pl.ds(i * size, size)], sems.at[i]
    )


def forward_kernel(strike_rows, ids_ref, model_hbm, green_ref, out_ref, gbuf, model_ref, cols, acc, model_sem, sems):
    slots, block = gbuf.shape[:2]
    windows = cols.shape[1]
    sta_rows, samples = out_ref.shape
    time_blocks = samples // block
    row_count = sta_rows * time_blocks
    size = slots // CHUNKS
    model_copy = pltpu.make_async_copy(model_hbm, model_ref, model_sem)
    model_copy.start()
    for i in range(CHUNKS):
        green_copy(green_ref, gbuf, sems, i, size).start()
    acc[...] = jnp.zeros_like(acc)
    model_copy.wait()
    for q in range(strike_rows):
        cols[q] = model_ref[pl.ds(q, windows, stride=strike_rows), :].astype(jnp.bfloat16)

    @pl.loop(0, CHUNKS)
    def _(i):
        green_copy(green_ref, gbuf, sems, i, size).wait()
        for u in range(size):
            c = i * size + u
            slot_id = ids_ref[c]
            safe = jnp.maximum(slot_id, 0)
            term = lax.dot_general(
                cols[lax.rem(safe, strike_rows)],
                gbuf[c],
                (((1,), (1,)), ((), ())),
                preferred_element_type=jnp.float32,
            )
            row = jnp.where(slot_id >= 0, lax.div(safe, strike_rows), row_count)
            acc[row] = acc[row] + term

    window = lax.broadcasted_iota(jnp.int32, (windows, block), 0)
    lane = lax.broadcasted_iota(jnp.int32, (windows, block), 1)
    same = lane >= window
    for a in range(sta_rows):
        before = jnp.zeros((windows, block), jnp.float32)
        for b in range(time_blocks):
            rolled = pltpu.roll(acc[a * time_blocks + b], 0, 1, stride=1, stride_axis=0)
            out_ref[a : a + 1, b * block : (b + 1) * block] = jnp.sum(
                jnp.where(same, rolled, before), axis=0, keepdims=True
            )
            before = rolled


def adjoint_kernel(strike_rows, ids_ref, synth_ref, data_ref, green_ref, resid_ref, acc, rows):
    slots, block = green_ref.shape[:2]
    windows = rows.shape[1]
    sta_rows, samples = resid_ref.shape
    time_blocks = samples // block
    size = slots // CHUNKS
    resid_ref[...] = synth_ref[...] - data_ref[...]
    acc[...] = jnp.zeros_like(acc)
    back = windows - 1 - lax.broadcasted_iota(jnp.int32, (windows, block), 0)
    same = lax.broadcasted_iota(jnp.int32, (windows, block), 1) + back < block
    for a in range(sta_rows):
        after = jnp.zeros((windows, block), jnp.float32)
        for b in reversed(range(time_blocks)):
            line = jnp.broadcast_to(resid_ref[a : a + 1, b * block : (b + 1) * block], (windows, block))
            rolled = pltpu.roll(line, block - windows + 1, 1, stride=1, stride_axis=0)
            rows[a * time_blocks + b] = jnp.where(same, rolled, after).astype(jnp.bfloat16)
            after = rolled

    @pl.loop(0, CHUNKS)
    def _(i):
        for u in range(size):
            c = i * size + u
            slot_id = ids_ref[c]
            safe = jnp.maximum(slot_id, 0)
            term = jnp.dot(
                rows[lax.div(safe, strike_rows)], green_ref[c], preferred_element_type=jnp.float32
            )
            q = jnp.where(slot_id >= 0, lax.rem(safe, strike_rows), strike_rows)
            here = pl.ds(pl.multiple_of(q * windows, windows), windows)
            acc[here, :] = acc[here, :] + term


def exchange_kernel(n, part_ref, out_ref, parts, send, recv):
    me = lax.axis_index("strike")
    barrier = pltpu.get_barrier_semaphore()
    for d in range(1, n):
        pl.semaphore_signal(
            barrier, inc=1, device_id={"strike": lax.rem(me + d, n)}, device_id_type=MESH
        )
    pl.semaphore_wait(barrier, n - 1)
    copies = []
    for d in range(1, n):
        copy = pltpu.make_async_remote_copy(
            src_ref=part_ref,
            dst_ref=parts.at[d],
            send_sem=send.at[d],
            recv_sem=recv.at[d],
            device_id={"strike": lax.rem(me + d, n)},
            device_id_type=MESH,
        )
        copy.start()
        copies.append(copy)
    parts[0] = part_ref[...]
    for copy in copies:
        copy.wait()
    total = parts[lax.rem(me, n)]
    for j in range(1, n):
        total = total + parts[lax.rem(me - j + n, n)]
    out_ref[...] = total


def reduce_kernel(
    n_sta, n_strike, acc_ref, out_ref, grad_ref, from_core, from_x, from_z, ext,
    core_s, core_r, x_s, x_r, z_s, z_r, halo_s, halo_r, gz_s, gz_r, gx_s, gx_r, gc_s, gc_r,
):
    depth = n_sta // 4
    own = grad_ref.shape[3]
    halves_of_rows = 2
    pieces = own * halves_of_rows
    rows, dip = grad_ref.shape[4:]
    part = rows // halves_of_rows
    sta = lax.axis_index("sta")
    strike = lax.axis_index("strike")
    core = lax.rem(sta, 2)
    x = lax.rem(lax.div(sta, 2), 2)
    z = lax.div(sta, 4)
    other_core, other_x = 1 - core, 1 - x
    core_dev = {"sta": z * 4 + x * 2 + other_core}
    x_dev = {"sta": z * 4 + other_x * 2 + core}

    def z_at(d):
        return lax.rem(z + d, depth)

    def z_dev(d):
        return {"sta": z_at(d) * 4 + x * 2 + core}

    up_dev = {"strike": lax.rem(strike + 1, n_strike)}
    down_dev = {"strike": lax.rem(strike + n_strike - 1, n_strike)}
    peers = [core_dev, x_dev] + [z_dev(d) for d in range(1, depth)] + [up_dev, down_dev]
    barrier = pltpu.get_barrier_semaphore()
    for peer in peers:
        pl.semaphore_signal(barrier, inc=1, device_id=peer, device_id_type=MESH)
    windows = 4 * depth * own
    for w in range(windows):
        place = (w // (windows // 2), w // (windows // 4) % 2, w // own % depth, w % own)
        grad_ref[place] = acc_ref[pl.ds(windows - 1 - w, rows, stride=windows), :]
    pl.semaphore_wait(barrier, len(peers))

    started = []

    def send(src, dst, s, r, dev):
        copy = pltpu.make_async_remote_copy(
            src_ref=src, dst_ref=dst, send_sem=s, recv_sem=r, device_id=dev, device_id_type=MESH
        )
        copy.start()
        started.append(copy)
        return copy

    def cut(k):
        return (pl.ds(k // halves_of_rows, 1), pl.ds(k % halves_of_rows * part, part))

    halves = []
    for h, side in enumerate((other_x, x)):
        for k in range(pieces):
            halves.append(
                send(
                    grad_ref.at[other_core, side, :, *cut(k)],
                    from_core.at[h, :, *cut(k)],
                    core_s.at[h, k],
                    core_r.at[h, k],
                    core_dev,
                )
            )
    across = []
    for k in range(pieces):
        halves[k].wait_recv()
        from_core[0, :, *cut(k)] = from_core[0, :, *cut(k)] + grad_ref[core, other_x, :, *cut(k)]
        across.append(
            send(from_core.at[0, :, *cut(k)], from_x.at[:, *cut(k)], x_s.at[k], x_r.at[k], x_dev)
        )
    for k in range(pieces):
        halves[pieces + k].wait_recv()
        from_core[1, :, *cut(k)] = from_core[1, :, *cut(k)] + grad_ref[core, x, :, *cut(k)]
    along = []
    for k in range(pieces):
        across[k].wait_recv()
        from_x[:, *cut(k)] = from_x[:, *cut(k)] + from_core[1, :, *cut(k)]
        for d in range(1, depth):
            along.append(
                send(
                    from_x.at[z_at(d), *cut(k)],
                    from_z.at[d - 1, *cut(k)],
                    z_s.at[d - 1, k],
                    z_r.at[d - 1, k],
                    z_dev(d),
                )
            )
    for copy in along:
        copy.wait_recv()
    field = from_x[z]
    for d in range(1, depth):
        field = field + from_z[d - 1]

    ext[:, HALO : HALO + rows] = field
    high = send(
        ext.at[:, pl.ds(rows, HALO)], ext.at[:, pl.ds(0, HALO)], halo_s.at[0], halo_r.at[0], up_dev
    )
    low = send(
        ext.at[:, pl.ds(HALO, HALO)],
        ext.at[:, pl.ds(HALO + rows, HALO)],
        halo_s.at[1],
        halo_r.at[1],
        down_dev,
    )

    def diffuse(v, inside):
        tall = v.shape[1]
        lane = lax.broadcasted_iota(jnp.int32, v.shape, 2)
        for _ in range(SWEEPS):
            left = jnp.where(lane > 0, pltpu.roll(v, 1, 2), 0.0)
            right = jnp.where(lane < dip - 1, pltpu.roll(v, dip - 1, 2), 0.0)
            around = pltpu.roll(v, tall - 1, 1) + pltpu.roll(v, 1, 1) + right + left - 4.0 * v
            v = v + NU_DIFF * around
            if inside is not None:
                v = jnp.where(inside, v, 0.0)
        return v

    mid = diffuse(field, None)
    out_ref[core, x, z, :, HALO : rows - HALO] = STEP_LEN * mid[:, HALO : rows - HALO]

    spans = ((HALO, rows - 2 * HALO), (0, HALO), (rows - HALO, HALO))

    def view(a, b, c, j):
        return out_ref.at[a, b, c, :, pl.ds(*spans[j])]

    fetched, crossed, to_core = {}, {}, []

    def give(j, d):
        block = view(core, x, lax.rem(z - d + depth, depth), j)
        crossed[j, d] = send(block, block, gx_s.at[j, d], gx_r.at[j, d], x_dev)
        to_core.append(send(block, block, gc_s.at[0, j, d], gc_r.at[0, j, d], core_dev))

    def spread(j):
        block = view(core, x, z, j)
        for d in range(1, depth):
            fetched[j, d] = send(block, block, gz_s.at[j, d], gz_r.at[j, d], z_dev(d))
        give(j, 0)

    spread(0)
    high.wait_recv()
    low.wait_recv()
    for j, start in ((1, 0), (2, rows - HALO)):
        strip = ext[:, start : start + 3 * HALO]
        row = lax.broadcasted_iota(jnp.int32, strip.shape, 1)
        if j == 1:
            inside = row >= jnp.where(strike > 0, 0, HALO)
        else:
            inside = row < jnp.where(strike < n_strike - 1, 3 * HALO, 2 * HALO)
        strip = diffuse(jnp.where(inside, strip, 0.0), inside)
        out_ref[core, x, z, :, spans[j][0] : spans[j][0] + HALO] = STEP_LEN * strip[:, HALO : 2 * HALO]
        spread(j)
    for j in range(3):
        for d in range(1, depth):
            fetched[j, d].wait_recv()
            give(j, d)
    for j in range(3):
        for d in range(depth):
            crossed[j, d].wait_recv()
            block = view(core, other_x, lax.rem(z - d + depth, depth), j)
            to_core.append(send(block, block, gc_s.at[1, j, d], gc_r.at[1, j, d], core_dev))
    for copy in to_core:
        copy.wait_recv()
    for copy in started:
        copy.wait_send()


def local(n_sta, n_strike, data, model, green, block_ids):
    sta_rows, samples = data.shape
    windows, strike_rows, dip = model.shape
    slots, block = green.shape[2], green.shape[3]
    row_count = sta_rows * (samples // block)
    green = green.reshape(green.shape[2:])
    ids = block_ids.reshape(-1)
    vmem = pl.BlockSpec(memory_space=pltpu.VMEM)
    smem = pl.BlockSpec(memory_space=pltpu.SMEM)
    hbm = pl.BlockSpec(memory_space=pl.ANY)
    f32 = jnp.float32
    dma = pltpu.SemaphoreType.DMA

    partial, green = pl.pallas_call(
        functools.partial(forward_kernel, strike_rows),
        out_shape=(
            jax.ShapeDtypeStruct((sta_rows, samples), f32),
            jax.ShapeDtypeStruct((slots, block, dip), green.dtype),
        ),
        in_specs=[smem, hbm, hbm],
        out_specs=(vmem, vmem),
        scratch_shapes=[
            pltpu.VMEM((windows * strike_rows, dip), f32),
            pltpu.VMEM((strike_rows, windows, dip), jnp.bfloat16),
            pltpu.VMEM((row_count + 1, windows, block), f32),
            dma,
            dma((CHUNKS,)),
        ],
        compiler_params=pltpu.CompilerParams(vmem_limit_bytes=VMEM_LIMIT),
        name="forward",
    )(
        ids,
        pltpu.with_memory_space_constraint(model.reshape(windows * strike_rows, dip), pltpu.HBM),
        pltpu.with_memory_space_constraint(green, pltpu.HBM),
    )

    synthetic = pl.pallas_call(
        functools.partial(exchange_kernel, n_strike),
        out_shape=jax.ShapeDtypeStruct((sta_rows, samples), f32),
        in_specs=[vmem],
        out_specs=vmem,
        scratch_shapes=[
            pltpu.VMEM((n_strike, sta_rows, samples), f32),
            dma((n_strike,)),
            dma((n_strike,)),
        ],
        compiler_params=pltpu.CompilerParams(collective_id=0, has_side_effects=True, vmem_limit_bytes=VMEM_LIMIT),
        name="exchange",
    )(partial)

    residual, grad = pl.pallas_call(
        functools.partial(adjoint_kernel, strike_rows),
        out_shape=(
            jax.ShapeDtypeStruct((sta_rows, samples), f32),
            jax.ShapeDtypeStruct(((strike_rows + 1) * windows, dip), f32),
        ),
        in_specs=[smem, vmem, vmem, vmem],
        out_specs=(vmem, vmem),
        scratch_shapes=[
            pltpu.VMEM((row_count, windows, block), jnp.bfloat16),
        ],
        compiler_params=pltpu.CompilerParams(vmem_limit_bytes=VMEM_LIMIT),
        name="adjoint",
    )(ids, synthetic, data, green)

    depth = n_sta // 4
    own = windows // n_sta
    pieces = 2 * own
    parted = (2, 2, depth, own, strike_rows, dip)
    field = pl.pallas_call(
        functools.partial(reduce_kernel, n_sta, n_strike),
        out_shape=jax.ShapeDtypeStruct(parted, f32),
        in_specs=[vmem],
        out_specs=vmem,
        scratch_shapes=[
            pltpu.VMEM(parted, f32),
            pltpu.VMEM((2,) + parted[2:], f32),
            pltpu.VMEM(parted[2:], f32),
            pltpu.VMEM((depth - 1,) + parted[3:], f32),
            pltpu.VMEM((own, strike_rows + 2 * HALO, dip), f32),
            dma((2, pieces)), dma((2, pieces)),
            dma((pieces,)), dma((pieces,)),
            dma((depth - 1, pieces)), dma((depth - 1, pieces)),
            dma((2,)), dma((2,)),
            dma((3, depth)), dma((3, depth)),
            dma((3, depth)), dma((3, depth)),
            dma((2, 3, depth)), dma((2, 3, depth)),
        ],
        compiler_params=pltpu.CompilerParams(collective_id=1, has_side_effects=True, vmem_limit_bytes=VMEM_LIMIT),
        name="reduce",
    )(grad)
    updated = model - field.reshape(windows, strike_rows, dip)
    return residual, updated


def solution(mesh):
    in_specs = (
        P("sta", None),
        P(None, "strike", None),
        P("sta", "strike", None, None, None),
        P("sta", "strike", None),
    )
    out_specs = (P("sta", None), P(None, "strike", None))
    body = functools.partial(local, mesh.shape["sta"], mesh.shape["strike"])
    return jax.shard_map(body, mesh=mesh, in_specs=in_specs, out_specs=out_specs, check_vma=False)
```
